256 devices in a mesh: depth: 4 (over z_lo), freq: 64 (over z_hi, x, y, core).
Axes of the slice: x: 4, y: 4, z: 8 (z_hi: 2, z_lo: 4; z = z_hi * 4 + z_lo), core: 2. Of those that a mesh axis runs over, the one named last changes fastest.
Arguments:
- source: float32 [64, 2, 256, 256], P('freq'), may hold values from -6 to 6
- receiver: float32 [64, 2, 256, 256], P('freq'), may hold values from -16 to 16
- classes: int32 [4, 256, 256], P('depth'), may hold values from 0 to 15
- coef_table: float32 [16, 64, 2, 6], replicated, may hold values from -2 to 2, as said below
- freq_list: int32 [64], P('freq'), may hold values from 0 to 63, each once
Outputs:
- image: float32 [256, 4, 8, 256], P('freq', 'depth')
The draws below stay inside these ranges and needn't reach their ends.
Inputs may be any that keep to these rules, and one draw needn't show every extreme that they name: `coef_table`: every entry lies within the stated bounds.
All inputs are finite; a program needn't handle non-finite values.
Results may differ from the reference program's by a relative error of at most 0.00011.
Values sent between devices are 32-bit elements; how exact they have to be, the bound alone decides.
No kernel may reach another device: no remote copies, remote signals or barrier semaphores. Data moves between devices by JAX's collectives and lax.ppermute only.
A program may use at most 64 MiB of HBM per device.

```python
import math
import jax
import jax.numpy as jnp

NX = 256
NY = 256
H = 8
K = 6
NCLASS = 16
F = 64
Z = 4


def draw_table(key, part):
    first, second, third = jax.random.split(jax.random.fold_in(key, 11), 3)
    slowness = jnp.exp(jax.random.uniform(first, (NCLASS,), jnp.float32, math.log(0.5), math.log(1.6)))
    omega = jax.random.uniform(second, (F,), jnp.float32, 0.3, 1.6)
    ratio = jax.random.uniform(third, (), jnp.float32, 0.8, 1.2)
    bound = slowness[:, None] * omega[None, :]
    nodes = 64
    angle = math.pi * (jnp.arange(nodes, dtype=jnp.float32) + 0.5) / nodes
    gap = angle[None, None, :] ** 2 - bound[:, :, None] ** 2
    phase = ratio * jnp.sqrt(jnp.maximum(-gap, 0.0))
    decay = jnp.exp(-ratio * jnp.sqrt(jnp.maximum(gap, 0.0)))
    value_real = jnp.where(gap < 0.0, jnp.cos(phase), decay)
    value_imag = jnp.where(gap < 0.0, jnp.sin(phase), 0.0)
    orders = jnp.arange(K, dtype=jnp.float32)
    basis = jnp.cos(orders[:, None] * angle[None, :])
    weights = jnp.where(orders == 0.0, 1.0, 2.0) / nodes
    coef_real = jnp.einsum('cgn,kn->cgk', value_real, basis) * weights
    coef_imag = jnp.einsum('cgn,kn->cgk', value_imag, basis) * weights
    fine = jnp.linspace(0.0, math.pi, 257)
    fine_basis = jnp.cos(orders[:, None] * fine[None, :])
    poly_real = jnp.einsum('cgk,kn->cgn', coef_real, fine_basis)
    poly_imag = jnp.einsum('cgk,kn->cgn', coef_imag, fine_basis)
    largest = jnp.max(jnp.sqrt(poly_real ** 2 + poly_imag ** 2 + 1e-12), axis=2)
    factor = 0.98 / largest
    table = jnp.stack([coef_real * factor[:, :, None], coef_imag * factor[:, :, None]], axis=2)
    return table.astype(jnp.float32)


def draw_coef_table(key, part):
    return draw_table(key, part)


def set_ends(values, stream_key, low, high):
    longest = values.shape.index(max(values.shape))
    spots = []
    for shift in (0, 1):
        where = [jax.random.randint(jax.random.fold_in(stream_key, axis), (), 0, length) for axis, length in enumerate(values.shape)]
        where[longest] = (where[longest] + shift) % values.shape[longest]
        spots.append(tuple(where))
    return values.at[spots[0]].set(low).at[spots[1]].set(high)


def strengthened(drawn, key, source, target, shards_of, factor):
    owner, partner = [(jnp.arange(drawn.shape[dim]) // (drawn.shape[dim] // shards_of)).reshape([-1 if axis == dim else 1 for axis in range(drawn.ndim)]) for dim in (source, target)]
    chosen = jax.random.permutation(key, shards_of)[partner]
    strong = (owner == chosen) | (owner == (partner + shards_of // 2) % shards_of)
    return jnp.where(strong, factor * drawn, drawn)


def levels(stream_key, shape, pieces, low, high):
    level = 1.0
    for position, parts in pieces:
        heights = jax.random.uniform(jax.random.fold_in(jax.random.fold_in(stream_key, 6), position), (parts,), jnp.float32, low / len(pieces), high / len(pieces))
        level = level * jnp.repeat(jnp.exp(heights), shape[position] // parts).reshape((-1,) + (1,) * (len(shape) - 1 - position))
    return level


def gaussian(stream_key, shape, scale, limit, cuts=(), kind=jnp.bfloat16):
    result = jax.random.normal(stream_key, shape, jnp.float32) * scale
    if len(cuts) > 0:
        result = levels(stream_key, shape, cuts, -0.22, 0.18) * result
    return jnp.clip(result, min=-limit, max=limit).astype(kind)


def bell_draw_with(own_key, dims, deviation, most, cuts, heavy, kind=jnp.bfloat16):
    result = deviation * jax.random.normal(own_key, dims, jnp.float32)
    if cuts:
        result = result * levels(own_key, dims, cuts, -0.22, 0.18)
    return jnp.clip(strengthened(result, jax.random.fold_in(own_key, 3), *heavy), -most, most).astype(kind)


def setup_inputs(seed: int = 0) -> dict:
    key_list = jax.random.split(jax.random.key(seed), 6)
    return {
        "source": gaussian(key_list[0], (F, 2, NX, NY), 1.0, 6.0, ((0, 64),), jnp.float32),
        "receiver": bell_draw_with(key_list[1], (F, 2, NX, NY), 1.0, 16.0, ((0, 64),), (0, 2, 64, 4.0), jnp.float32),
        "classes": set_ends(jax.random.randint(key_list[2], (Z, NX, NY), 0, NCLASS), jax.random.fold_in(key_list[2], 1), 0, NCLASS - 1).astype(jnp.int32),
        "coef_table": draw_coef_table(jax.random.fold_in(key_list[5], 71), 0),
        "freq_list": jax.random.permutation(key_list[4], F).astype(jnp.int32),
    }


def mcclellan(field):
    widths = [(0, 0)] * (field.ndim - 2) + [(1, 1), (1, 1)]
    padded = jnp.pad(field, widths)
    axial_sum = padded[..., 2:, 1:-1] + padded[..., :-2, 1:-1] + padded[..., 1:-1, 2:] + padded[..., 1:-1, :-2]
    corner_sum = padded[..., 2:, 2:] + padded[..., 2:, :-2] + padded[..., :-2, 2:] + padded[..., :-2, :-2]
    return -0.5 * field + 0.25 * axial_sum + 0.125 * corner_sum


def extrapolate(fields, coeffs):
    terms = coeffs.shape[3]
    earlier = fields
    current = mcclellan(fields)
    total_real = coeffs[:, :, 0, 0] * earlier[:, :, 0] - coeffs[:, :, 1, 0] * earlier[:, :, 1]
    total_imag = coeffs[:, :, 0, 0] * earlier[:, :, 1] + coeffs[:, :, 1, 0] * earlier[:, :, 0]
    for term_no in range(1, terms):
        total_real = total_real + coeffs[:, :, 0, term_no] * current[:, :, 0] - coeffs[:, :, 1, term_no] * current[:, :, 1]
        total_imag = total_imag + coeffs[:, :, 0, term_no] * current[:, :, 1] + coeffs[:, :, 1, term_no] * current[:, :, 0]
        if term_no + 1 < terms:
            following = 2.0 * mcclellan(current) - earlier
            earlier, current = current, following
    return jnp.stack([total_real, total_imag], axis=2)


def reference(source, receiver, classes, coef_table, freq_list):
    chosen = jnp.take(coef_table, freq_list, axis=1)
    chosen = jnp.transpose(chosen, (1, 2, 3, 0))
    imag_sign = jnp.array([1.0, -1.0], dtype=chosen.dtype)
    both_tables = jnp.stack([chosen * imag_sign[None, :, None, None], chosen])
    fields = jnp.stack([source, receiver])
    margin = H // 2
    scaling = F ** -0.5
    per_level = []
    for level in range(Z):
        coeffs = jnp.take(both_tables, classes[level], axis=4)
        fields = extrapolate(fields, coeffs)
        padded = jnp.pad(fields, [(0, 0), (0, 0), (0, 0), (margin, margin), (0, 0)])
        offsets = []
        for offset_no in range(H):
            shift_x = offset_no - margin
            src_part = padded[0, :, :, margin - shift_x:margin - shift_x + NX]
            rec_part = padded[1, :, :, margin + shift_x:margin + shift_x + NX]
            offsets.append(jnp.sum(src_part * rec_part, axis=(0, 1)))
        per_level.append(jnp.stack(offsets, axis=1))
    return jnp.stack(per_level, axis=1) * scaling
```

```python
import functools
import jax
import jax.numpy as jnp
from jax import lax
from jax.experimental import pallas as pl
from jax.experimental.pallas import tpu as pltpu
from jax.sharding import PartitionSpec as P

AXES = ("depth", "freq")
H = 8
K = 6
Z = 4
NX = 256
NY = 256
CHUNK = 64
WIN = 112
HALO = 24
STEPS = WIN // 8
EXT = STEPS + 8
LANES = 128
HALVES = NY // LANES


def split(linear):
    d, f = divmod(linear, 64)
    return d, f >> 5, (f >> 3) & 3, (f >> 1) & 3, f & 1


def join(d, zh, x, y, c):
    return d * 64 + ((zh * 4 + x) * 4 + y) * 2 + c


def route(move):
    return [(i, join(*move(*split(i)))) for i in range(256)]


def along_z(step):
    def move(d, zh, x, y, c):
        z = (zh * 4 + d + step(c)) % 8
        return z & 3, z >> 2, x, y, c

    return route(move)


def first_axis(t):
    def move(d, zh, x, y, c):
        return (d, zh, (x + t) % 4, y, c) if c == 0 else (d, zh, x, (y + t) % 4, c)

    return route(move)


def second_axis(t):
    def move(d, zh, x, y, c):
        return (d, zh, x, (y + t) % 4, c) if c == 0 else (d, zh, (x + t) % 4, y, c)

    return route(move)


def to_owner(p):
    def move(q, zh, x, y, c):
        level = 2 * (p ^ zh) + ((x >> 1) ^ (q & 1))
        return level, q >> 1, 2 * (q & 1) + (x & 1), y, c

    return route(move)


CORE_SWAP = route(lambda d, zh, x, y, c: (d, zh, x, y, 1 - c))


def window_start(q):
    return jnp.clip(CHUNK * q - HALO, 0, NX - WIN)


def kernel(place, src, rec, c0, c1, c2, c3, table, out, raw, cls, field, terms, img, in_sem, cls_sem, out_sem):
    q, x_at, y_at, core = place[0], place[1], place[2], place[3]
    start = pl.multiple_of(place[4], 8)
    loads = []
    for n, ref in enumerate((src, rec)):
        for half in range(HALVES):
            lanes = pl.ds(half * LANES, LANES)
            cp = pltpu.make_async_copy(ref.at[0, :, pl.ds(start, WIN), lanes], raw.at[n, :, half], in_sem.at[n, half])
            cp.start()
            loads.append(cp)
    cls_loads = []
    for n, ref in enumerate((c0, c1, c2, c3)):
        for half in range(HALVES):
            lanes = pl.ds(half * LANES, LANES)
            cp = pltpu.make_async_copy(ref.at[:, lanes], cls.at[place[5 + n], half], cls_sem.at[n, half])
            cp.start()
            cls_loads.append(cp)
    for cp in loads:
        cp.wait()

    lane = lax.broadcasted_iota(jnp.int32, (8, LANES), 1)
    sub = lax.broadcasted_iota(jnp.int32, (8, LANES), 0)
    first_lane, last_lane = lane == 0, lane == LANES - 1
    zero = jnp.zeros((8, LANES), jnp.float32)

    def from_above(v):
        return jnp.where(sub == 0, 0.0, pltpu.roll(v, 1, 0))

    def from_below(v):
        return jnp.where(sub == 7, 0.0, pltpu.roll(v, 7, 0))

    def left(lo, hi):
        rl, rh = pltpu.roll(lo, 1, 1), pltpu.roll(hi, 1, 1)
        return jnp.where(first_lane, zero, rl), jnp.where(first_lane, rl, rh)

    def right(lo, hi):
        rl, rh = pltpu.roll(lo, LANES - 1, 1), pltpu.roll(hi, LANES - 1, 1)
        return jnp.where(last_lane, rh, rl), jnp.where(last_lane, zero, rh)

    for comp in range(4):
        for r in range(STEPS):
            for half in range(HALVES):
                v = raw[comp // 2, comp % 2, half, pl.ds(r, 8, stride=STEPS), :]
                field[comp, half, 4 + r] = -v if comp == 1 else v
    for cp in cls_loads:
        cp.wait()

    def piece_copy(level, slot, i):
        c_o, y_o, ix = i & 1, (i >> 1) & 3, i >> 3
        lb, e = level >> 1, level & 1
        x_o = 2 * (e ^ (q & 1)) + ix
        dx, dy = (x_o - x_at) & 3, (y_o - y_at) & 3
        t, u = (dx, dy) if c_o == 0 else (dy, dx)
        at = (((c_o ^ core) * 4 + t) * 4 + u) * 2 + lb
        rows = pl.multiple_of((CHUNK * q - start + 4 * i) * H, 32)
        return pltpu.make_async_copy(img.at[slot, :, pl.ds(rows, 4 * H), :], out.at[at], out_sem.at[slot])

    def level_body(level, carry):
        slot = level & 1

        for k in range(1, K):
            for comp in range(4):
                def cur(r, half):
                    return field[comp, half, 4 + r] if k == 1 else terms[k - 2, comp, half, r]

                prev = [None, None]
                here = [cur(0, half) for half in range(HALVES)]
                above = [from_above(cur(STEPS - 1, half)) for half in range(HALVES)]
                top = here
                for r in range(STEPS):
                    if r < STEPS - 1:
                        below = [cur(r + 1, half) for half in range(HALVES)]
                    else:
                        below = [from_below(v) for v in top]
                    g, rest = [], []
                    for half in range(HALVES):
                        h = 0.5 * (above[half] + below[half])
                        g.append(h + here[half])
                        rest.append(h - here[half])
                    gl, gr = left(*g), right(*g)
                    for half in range(HALVES):
                        w = 0.5 * (gl[half] + gr[half]) + rest[half]
                        if k == 1:
                            w = 0.5 * w
                        elif k == 2:
                            w = w - field[comp, half, 4 + r]
                        else:
                            w = w - terms[k - 3, comp, half, r]
                        terms[k - 1, comp, half, r] = w
                    above, here = here, below

        def combine(r, carry):
            for half in range(HALVES):
                ids = cls[level, half, pl.ds(r, 8, stride=STEPS), :]
                coef = [
                    jnp.take_along_axis(table[n], ids, axis=1, mode="promise_in_bounds") for n in range(2 * K)
                ]
                p, s = [], []
                for comp in range(4):
                    vals = [field[comp, half, 4 + r]] + [terms[k, comp, half, r] for k in range(K - 1)]
                    a, b = coef[0] * vals[0], coef[K] * vals[0]
                    for k in range(1, K):
                        a = a + coef[k] * vals[k]
                        b = b + coef[K + k] * vals[k]
                    p.append(a)
                    s.append(b)
                for pair in range(2):
                    field[2 * pair, half, 4 + r] = p[2 * pair] - s[2 * pair + 1]
                    field[2 * pair + 1, half, 4 + r] = p[2 * pair + 1] + s[2 * pair]
            return carry

        lax.fori_loop(0, STEPS, combine, 0)
        for comp in range(4):
            for half in range(HALVES):
                for r in range(4):
                    field[comp, half, r] = from_above(field[comp, half, STEPS + r])
                    field[comp, half, STEPS + 4 + r] = from_below(field[comp, half, 4 + r])

        @pl.when(level >= 2)
        def _():
            for i in range(16):
                piece_copy(level - 2, slot, i).wait()

        def image(r, carry):
            for half in range(HALVES):
                for j in range(H):
                    h = j - H // 2
                    a = 4 + r - h
                    b = 4 + r + h
                    val = field[0, half, a] * field[2, half, b] - field[1, half, a] * field[3, half, b]
                    img[slot, half, pl.ds(r * H + j, 8, stride=STEPS * H), :] = val
            return carry

        lax.fori_loop(0, STEPS, image, 0)
        for i in range(16):
            piece_copy(level, slot, i).start()
        return carry

    lax.fori_loop(0, Z, level_body, 0)
    for level in (Z - 2, Z - 1):
        for i in range(16):
            piece_copy(level, level & 1, i).wait()


def images(place, source, receiver, class_windows, table):
    anyspace = pl.BlockSpec(memory_space=pl.ANY)
    return pl.pallas_call(
        kernel,
        out_shape=jax.ShapeDtypeStruct((64, HALVES, 4 * H, LANES), jnp.float32),
        in_specs=[pl.BlockSpec(memory_space=pltpu.SMEM)] + [anyspace] * 6 + [pl.BlockSpec(memory_space=pltpu.VMEM)],
        out_specs=anyspace,
        scratch_shapes=[
            pltpu.VMEM((2, 2, HALVES, WIN, LANES), jnp.float32),
            pltpu.VMEM((Z, HALVES, WIN, LANES), jnp.int32),
            pltpu.VMEM((4, HALVES, EXT, 8, LANES), jnp.float32),
            pltpu.VMEM((K - 1, 4, HALVES, STEPS, 8, LANES), jnp.float32),
            pltpu.VMEM((2, HALVES, WIN * H, LANES), jnp.float32),
            pltpu.SemaphoreType.DMA((2, HALVES)),
            pltpu.SemaphoreType.DMA((4, HALVES)),
            pltpu.SemaphoreType.DMA((2,)),
        ],
    )(place, source, receiver, *class_windows, table)


def per_device(source, receiver, classes, coef_table, freq_list):
    q = lax.axis_index("depth")
    f = lax.axis_index("freq")
    zh, x_at, y_at, core = f >> 5, (f >> 3) & 3, (f >> 1) & 3, f & 1

    def window(target):
        return lax.dynamic_slice(classes[0], (window_start(target & 3), 0), (WIN, NY))

    opposite = window(q + 2)
    class_windows = [
        window(q),
        lax.ppermute(window(q + 1), AXES, along_z(lambda c: 1)),
        lax.ppermute(window(q - 1), AXES, along_z(lambda c: -1)),
        lax.ppermute(opposite, AXES, along_z(lambda c: 2 if c == 0 else -2)),
    ]
    levels = [q, (q - 1) & 3, (q + 1) & 3, (q + 2) & 3]
    mine = lax.dynamic_slice_in_dim(coef_table, freq_list[0], 1, axis=1)[:, 0]
    rows = jnp.transpose(mine, (1, 2, 0)).reshape(2 * K, 1, -1)
    table = jnp.broadcast_to(jnp.pad(rows, [(0, 0), (0, 0), (0, LANES - rows.shape[2])]), (2 * K, 8, LANES))
    place = jnp.stack([q, x_at, y_at, core, window_start(q)] + levels).astype(jnp.int32)
    terms = images(place, source, receiver, class_windows, table)

    mine = terms[:32] + lax.ppermute(terms[32:], AXES, CORE_SWAP)
    for axis in (first_axis, second_axis):
        part = mine.shape[0] // 4
        got = [lax.ppermute(mine[t * part : (t + 1) * part], AXES, axis(t)) for t in (1, 2, 3)]
        mine = mine[:part] + got[0] + got[1] + got[2]
    sent = [lax.dynamic_index_in_dim(mine, p ^ zh, 0, keepdims=False) for p in (0, 1)]
    total = lax.ppermute(sent[0], AXES, to_owner(0)) + lax.ppermute(sent[1], AXES, to_owner(1))
    scaling = 64.0 ** -0.5
    image = (total * scaling).reshape(HALVES, 4, H, LANES)
    return jnp.transpose(image, (1, 2, 0, 3)).reshape(4, 1, H, NY)


def solution(mesh):
    placed = (
        P("freq", None, None, None),
        P("freq", None, None, None),
        P("depth", None, None),
        P(),
        P("freq"),
    )
    return jax.shard_map(
        per_device,
        mesh=mesh,
        in_specs=placed,
        out_specs=P("freq", "depth", None, None),
        check_vma=False,
    )
```

```python
import functools
import jax
import jax.numpy as jnp
from jax import lax
from jax.experimental import pallas as pl
from jax.experimental.pallas import tpu as pltpu
from jax.sharding import PartitionSpec as P

AXES = ("depth", "freq")
H = 8
K = 6
Z = 4
NX = 256
NY = 256
CHUNK = 64
WIN = 112
HALO = 24
STEPS = WIN // 8
PAD = 8
ROWS = WIN + 2 * PAD
COMBINE = 7
IMAGE = 4
SKEW = 3
COMPS = 2
LIMIT = 32
LANES = 128
HALVES = NY // LANES


def split(linear):
    d, f = divmod(linear, 64)
    return d, f >> 5, (f >> 3) & 3, (f >> 1) & 3, f & 1


def join(d, zh, x, y, c):
    return d * 64 + ((zh * 4 + x) * 4 + y) * 2 + c


def route(move):
    return [(i, join(*move(*split(i)))) for i in range(256)]


def along_z(step):
    def move(d, zh, x, y, c):
        z = (zh * 4 + d + step(c)) % 8
        return z & 3, z >> 2, x, y, c

    return route(move)


def first_axis(t):
    def move(d, zh, x, y, c):
        return (d, zh, (x + t) % 4, y, c) if c == 0 else (d, zh, x, (y + t) % 4, c)

    return route(move)


def second_axis(t):
    def move(d, zh, x, y, c):
        return (d, zh, x, (y + t) % 4, c) if c == 0 else (d, zh, (x + t) % 4, y, c)

    return route(move)


def to_owner(p):
    def move(q, zh, x, y, c):
        far = (x >> 1) ^ (q & 1)
        return 2 * (p ^ zh) + (x >> 1), q >> 1, 2 * (q & 1) + ((x & 1) ^ far), y, c

    return route(move)


CORE_SWAP = route(lambda d, zh, x, y, c: (d, zh, x, y, 1 - c))


def window_start(q):
    return jnp.clip(CHUNK * q - HALO, 0, NX - WIN)


def lanes_of(shape=(8, LANES)):
    return lax.broadcasted_iota(jnp.int32, shape, 1)


def pick(v, ids, axis=1):
    return jnp.take_along_axis(v, ids, axis=axis, mode="promise_in_bounds")


def by_parity(lo, hi):
    lane = lanes_of()
    even = (2 * lane) & (LANES - 1)
    low = lane < LANES // 2
    return tuple(jnp.where(low, pick(lo, even + p), pick(hi, even + p)) for p in (0, 1))


def by_column(even, odd):
    lane = lanes_of()
    is_odd = (lane & 1) == 1
    return tuple(
        jnp.where(is_odd, pick(odd, (lane >> 1) + base), pick(even, (lane >> 1) + base)) for base in (0, LANES // 2)
    )


def cut_windows(place, classes, own, two, up, down, raw, parted, sem):
    quarter = NX // 4
    loads = []
    for n in range(4):
        rows = pl.ds(quarter * n, quarter)
        cp = pltpu.make_async_copy(classes.at[0, rows, :], raw.at[rows, :], sem.at[n])
        cp.start()
        loads.append(cp)
    for n in range(4):
        loads[n].wait()
        for r in range(quarter * n, quarter * (n + 1), 8):
            for half, v in enumerate(by_parity(raw[r : r + 8, 0:LANES], raw[r : r + 8, LANES:NY])):
                parted[half, r : r + 8, :] = v
    for n, ref in enumerate((own, two, up, down)):
        start = pl.multiple_of(place[4 + n], 8)
        for half in range(HALVES):
            for tile in range(STEPS):
                ref[half, 8 * tile : 8 * tile + 8, :] = parted[half, pl.ds(start + 8 * tile, 8), :]


def stencil(field, comp):
    lane = lanes_of()
    first_lane, last_lane = lane == 0, lane == LANES - 1
    for step in range(STEPS + SKEW * (K - 2)):
        for k in range(1, K):
            tile = step - SKEW * (k - 1)
            if not 0 <= tile < STEPS:
                continue
            r = PAD + 8 * tile
            g, rest = [], []
            for half in range(HALVES):
                v = field[k - 1, comp, half, r : r + 8, :]
                h = 0.5 * (field[k - 1, comp, half, r - 1 : r + 7, :] + field[k - 1, comp, half, r + 1 : r + 9, :])
                g.append(h + v)
                rest.append(h - v)
            before = jnp.where(first_lane, 0.0, pltpu.roll(g[1], 1, 1))
            after = jnp.where(last_lane, 0.0, pltpu.roll(g[0], LANES - 1, 1))
            sides = (before + g[1], g[0] + after)
            for half in range(HALVES):
                w = 0.5 * sides[half] + rest[half]
                if k == 1:
                    w = 0.5 * w
                else:
                    w = w - field[k - 2, comp, half, r : r + 8, :]
                field[k, comp, half, r : r + 8, :] = w


def stencils(field):
    def some(step, carry):
        for part in range(COMPS):
            stencil(field, COMPS * step + part)
        return carry

    lax.fori_loop(0, 4 // COMPS, some, 0)


def clear_ends(field):
    zero = jnp.zeros((8, LANES), jnp.float32)
    for k in range(K - 1):
        for comp in range(4):
            for half in range(HALVES):
                field[k, comp, half, 0:PAD, :] = zero
                field[k, comp, half, PAD + WIN : ROWS, :] = zero


def first_terms(place, src, rec, field, raw, sem):
    start = pl.multiple_of(place[4], 8)
    loads = []
    for n, ref in enumerate((src, rec)):
        cp = pltpu.make_async_copy(ref.at[0, :, pl.ds(start, WIN), :], raw.at[n], sem.at[n])
        cp.start()
        loads.append(cp)
    clear_ends(field)
    for n in range(2):
        loads[n].wait()
        for part in range(2):
            for tile in range(STEPS):
                r = 8 * tile
                lo, hi = raw[n, part, r : r + 8, 0:LANES], raw[n, part, r : r + 8, LANES:NY]
                for half, v in enumerate(by_parity(lo, hi)):
                    field[0, 2 * n + part, half, PAD + r : PAD + r + 8, :] = v
    stencils(field)


def all_levels(place, first, w0, w1, w2, w3, coef, keep, send, field, cls, table):
    q, x_at, y_at, core = place[0], place[1], place[2], place[3]
    for n, ref in enumerate((w0, w1, w2, w3)):
        level = place[8 + n]
        for half in range(HALVES):
            for tile in range(STEPS):
                cls[level, half, 8 * tile : 8 * tile + 8, :] = ref[half, 8 * tile : 8 * tile + 8, :]
    clear_ends(field)
    for n in range(2 * K):
        table[n] = jnp.broadcast_to(coef[n : n + 1, :], (8, LANES))
    mirror = 7 - lax.broadcasted_iota(jnp.int32, (8, LANES), 0)
    base = pl.multiple_of(PAD + CHUNK * q - place[4], 8)

    def finish(level, terms):
        def combine(step, carry):
            places = []
            for part in range(COMBINE):
                r = pl.multiple_of(PAD + 8 * (COMBINE * step + part), 8)
                places += [(half, r) for half in range(HALVES)]

            def look_up(half, r):
                ids = cls[level, half, pl.ds(r - PAD, 8), :]
                return [pick(table[n], ids) for n in range(2 * K)]

            ahead = look_up(*places[0])
            for n, (half, r) in enumerate(places):
                coefs = ahead
                if n + 1 < len(places):
                    ahead = look_up(*places[n + 1])
                p, s = [], []
                for comp in range(4):
                    vals = [terms[k, comp, half, pl.ds(r, 8), :] for k in range(K)]
                    a, b = coefs[0] * vals[0], coefs[K] * vals[0]
                    for k in range(1, K):
                        a = a + coefs[k] * vals[k]
                        b = b + coefs[K + k] * vals[k]
                    p.append(a)
                    s.append(b)
                field[0, 0, half, pl.ds(r, 8), :] = p[0] + s[1]
                field[0, 1, half, pl.ds(r, 8), :] = p[1] - s[0]
                field[0, 2, half, pl.ds(r, 8), :] = p[2] - s[3]
                field[0, 3, half, pl.ds(r, 8), :] = p[3] + s[2]
            return carry

        lax.fori_loop(0, STEPS // COMBINE, combine, 0)
        lb, e = level >> 1, level & 1

        def image(step, carry):
            for part in range(IMAGE):
                image_rows(IMAGE * step + part)
            return carry

        def image_rows(m):
            y_o, ix = m & 3, m >> 2
            x_o = 2 * e + (ix ^ e ^ (q & 1))
            dx, dy = (x_o - x_at) & 3, (y_o - y_at) & 3
            for flip, ref in enumerate((keep, send)):
                c_o = core ^ flip
                t = jnp.where(c_o == 0, dx, dy)
                u = jnp.where(c_o == 0, dy, dx)
                at = (t * 4 + u) * 2 + lb
                for row in range(4):
                    x = base + 4 * (2 * m + c_o) + row
                    for half in range(HALVES):
                        s_re, s_im = [pick(field[0, comp, half, pl.ds(x - 3, 8), :], mirror, 0) for comp in (0, 1)]
                        r_re, r_im = [field[0, comp, half, pl.ds(x - 4, 8), :] for comp in (2, 3)]
                        ref[at, half, H * row : H * row + H, :] = s_re * r_re + s_im * r_im

        lax.fori_loop(0, 8 // IMAGE, image, 0)

    finish(0, first)

    def level_body(level, carry):
        stencils(field)
        finish(level, field)
        return carry

    lax.fori_loop(1, Z, level_body, 0)


def last_sum(a, b, out):
    scaling = 64.0 ** -0.5
    for tile in range(4):
        rows = slice(8 * tile, 8 * tile + 8)
        parts = [(a[half, rows, :] + b[half, rows, :]) * scaling for half in range(HALVES)]
        lo, hi = by_column(*parts)
        out[tile, 0, :, 0:LANES] = lo
        out[tile, 0, :, LANES:NY] = hi


SCALARS = pl.BlockSpec(memory_space=pltpu.SMEM)
LOCAL = pl.BlockSpec(memory_space=pltpu.VMEM)
REMOTE = pl.BlockSpec(memory_space=pltpu.HBM)
TERMS = (K, 4, HALVES, ROWS, LANES)
WINDOW = (HALVES, WIN, LANES)


def call(body, outs, ins, scratch=(), flops=0, moved=0):
    return pl.pallas_call(
        body,
        out_shape=[jax.ShapeDtypeStruct(shape, dtype) for shape, dtype in outs],
        in_specs=ins,
        out_specs=[LOCAL] * len(outs),
        scratch_shapes=list(scratch),
        cost_estimate=pl.CostEstimate(flops=flops, bytes_accessed=moved, transcendentals=0),
        compiler_params=pltpu.CompilerParams(vmem_limit_bytes=LIMIT * 2**20),
    )


def per_device(source, receiver, classes, coef_table, freq_list):
    q = lax.axis_index("depth")
    f = lax.axis_index("freq")
    zh, x_at, y_at, core = f >> 5, (f >> 3) & 3, (f >> 1) & 3, f & 1
    starts = [window_start((q + step) & 3) for step in (0, 2, 1, -1)]
    levels = [(q + step) & 3 for step in (0, 2, -1, 1)]
    place = jnp.stack([q, x_at, y_at, core] + starts + levels).astype(jnp.int32)
    own, two, up, down = call(
        cut_windows,
        [(WINDOW, jnp.int32)] * 4,
        [SCALARS, REMOTE],
        [pltpu.VMEM((NX, NY), jnp.int32), pltpu.VMEM((HALVES, NX, LANES), jnp.int32), pltpu.SemaphoreType.DMA((4,))],
    )(place, classes)
    class_windows = [
        own,
        lax.ppermute(two, AXES, along_z(lambda c: 2 if c == 0 else -2)),
        lax.ppermute(up, AXES, along_z(lambda c: 1)),
        lax.ppermute(down, AXES, along_z(lambda c: -1)),
    ]
    mine = lax.dynamic_slice_in_dim(coef_table, freq_list[0], 1, axis=1)[:, 0]
    rows = jnp.transpose(mine, (1, 2, 0)).reshape(2 * K, -1)
    coef = jnp.pad(rows, [(0, 4), (0, LANES - rows.shape[1])])
    (first,) = call(
        first_terms,
        [(TERMS, jnp.float32)],
        [SCALARS, REMOTE, REMOTE],
        [pltpu.VMEM((2, 2, WIN, NY), jnp.float32), pltpu.SemaphoreType.DMA((2,))],
        flops=10**7,
        moved=4 * 2**20,
    )(place, source, receiver)
    half_image = ((32, HALVES, 4 * H, LANES), jnp.float32)
    keep, send = call(
        all_levels,
        [half_image, half_image],
        [SCALARS] + [LOCAL] * 6,
        [
            pltpu.VMEM(TERMS, jnp.float32),
            pltpu.VMEM((Z,) + WINDOW, jnp.int32),
            pltpu.VMEM((2 * K, 8, LANES), jnp.float32),
        ],
        flops=5 * 10**7,
        moved=4 * 2**20,
    )(place, first, *class_windows, coef)

    mine = keep + lax.ppermute(send, AXES, CORE_SWAP)
    for axis in (first_axis, second_axis):
        part = mine.shape[0] // 4
        got = [lax.ppermute(mine[t * part : (t + 1) * part], AXES, axis(t)) for t in (1, 2, 3)]
        mine = mine[:part] + got[0] + got[1] + got[2]
    sent = [lax.dynamic_index_in_dim(mine, p ^ zh, 0, keepdims=False) for p in (0, 1)]
    got = [lax.ppermute(sent[p], AXES, to_owner(p)) for p in (0, 1)]
    (image,) = call(last_sum, [((4, 1, H, NY), jnp.float32)], [LOCAL, LOCAL])(*got)
    return image


def solution(mesh):
    placed = (
        P("freq", None, None, None),
        P("freq", None, None, None),
        P("depth", None, None),
        P(),
        P("freq"),
    )
    return jax.shard_map(
        per_device,
        mesh=mesh,
        in_specs=placed,
        out_specs=P("freq", "depth", None, None),
        check_vma=False,
    )
```

```python
import functools
import jax
import jax.numpy as jnp
from jax import lax
from jax.experimental import pallas as pl
from jax.experimental.pallas import tpu as pltpu
from jax.sharding import PartitionSpec as P

AXES = ("depth", "freq")
H = 8
K = 6
Z = 4
NX = 256
NY = 256
CHUNK = 64
WIN = 112
HALO = 24
STEPS = WIN // 8
PAD = 8
ROWS = WIN + 2 * PAD
COMBINE = 7
IMAGE = 4
SKEW = 3
COMPS = 2
LIMIT = 32
LANES = 128
HALVES = NY // LANES


def split(linear):
    d, f = divmod(linear, 64)
    return d, f >> 5, (f >> 3) & 3, (f >> 1) & 3, f & 1


def join(d, zh, x, y, c):
    return d * 64 + ((zh * 4 + x) * 4 + y) * 2 + c


def route(move):
    return [(i, join(*move(*split(i)))) for i in range(256)]


def along_z(step):
    def move(d, zh, x, y, c):
        z = (zh * 4 + d + step(c)) % 8
        return z & 3, z >> 2, x, y, c

    return route(move)


def first_axis(t):
    def move(d, zh, x, y, c):
        return (d, zh, (x + t) % 4, y, c) if c == 0 else (d, zh, x, (y + t) % 4, c)

    return route(move)


def second_axis(t):
    def move(d, zh, x, y, c):
        return (d, zh, x, (y + t) % 4, c) if c == 0 else (d, zh, (x + t) % 4, y, c)

    return route(move)


def chunk_at(z):
    return ((z & 3) + 2 * (z >> 2) + 3) & 3


def sent_first(q, zh):
    return 1 ^ zh ^ (q & 1) ^ (q >> 1)


def to_owner(p):
    def move(d, zh, x, y, c):
        q = chunk_at(4 * zh + d)
        e = (x >> 1) ^ (q & 1)
        level = e ^ (3 * (p ^ sent_first(q, zh)))
        return level, q >> 1, 2 * (q & 1) + ((x & 1) ^ e), y, c

    return route(move)


CORE_SWAP = route(lambda d, zh, x, y, c: (d, zh, x, y, 1 - c))


def window_start(q):
    return jnp.clip(CHUNK * q - HALO, 0, NX - WIN)


def lanes_of(shape=(8, LANES)):
    return lax.broadcasted_iota(jnp.int32, shape, 1)


def pick(v, ids, axis=1):
    return jnp.take_along_axis(v, ids, axis=axis, mode="promise_in_bounds")


def by_parity(lo, hi):
    lane = lanes_of()
    even = (2 * lane) & (LANES - 1)
    low = lane < LANES // 2
    return tuple(jnp.where(low, pick(lo, even + p), pick(hi, even + p)) for p in (0, 1))


def by_column(even, odd):
    lane = lanes_of()
    is_odd = (lane & 1) == 1
    return tuple(
        jnp.where(is_odd, pick(odd, (lane >> 1) + base), pick(even, (lane >> 1) + base)) for base in (0, LANES // 2)
    )


def cut_windows(place, classes, own, two, up, down, raw, parted, sem):
    quarter = NX // 4
    loads = []
    for n in range(4):
        rows = pl.ds(quarter * n, quarter)
        cp = pltpu.make_async_copy(classes.at[0, rows, :], raw.at[rows, :], sem.at[n])
        cp.start()
        loads.append(cp)
    for n in range(4):
        loads[n].wait()
        for r in range(quarter * n, quarter * (n + 1), 8):
            for half, v in enumerate(by_parity(raw[r : r + 8, 0:LANES], raw[r : r + 8, LANES:NY])):
                parted[half, r : r + 8, :] = v
    for n, ref in enumerate((own, two, up, down)):
        start = pl.multiple_of(place[4 + n], 8)
        for half in range(HALVES):
            for tile in range(STEPS):
                ref[half, 8 * tile : 8 * tile + 8, :] = parted[half, pl.ds(start + 8 * tile, 8), :]


def stencil(field, comp):
    lane = lanes_of()
    first_lane, last_lane = lane == 0, lane == LANES - 1
    for step in range(STEPS + SKEW * (K - 2)):
        for k in range(1, K):
            tile = step - SKEW * (k - 1)
            if not 0 <= tile < STEPS:
                continue
            r = PAD + 8 * tile
            g, rest = [], []
            for half in range(HALVES):
                v = field[k - 1, comp, half, r : r + 8, :]
                h = 0.5 * (field[k - 1, comp, half, r - 1 : r + 7, :] + field[k - 1, comp, half, r + 1 : r + 9, :])
                g.append(h + v)
                rest.append(h - v)
            before = jnp.where(first_lane, 0.0, pltpu.roll(g[1], 1, 1))
            after = jnp.where(last_lane, 0.0, pltpu.roll(g[0], LANES - 1, 1))
            sides = (before + g[1], g[0] + after)
            for half in range(HALVES):
                w = 0.5 * sides[half] + rest[half]
                if k == 1:
                    w = 0.5 * w
                else:
                    w = w - field[k - 2, comp, half, r : r + 8, :]
                field[k, comp, half, r : r + 8, :] = w


def stencils(field):
    def some(step, carry):
        for part in range(COMPS):
            stencil(field, COMPS * step + part)
        return carry

    lax.fori_loop(0, 4 // COMPS, some, 0)


def clear_ends(field):
    zero = jnp.zeros((8, LANES), jnp.float32)
    for k in range(K - 1):
        for comp in range(4):
            for half in range(HALVES):
                field[k, comp, half, 0:PAD, :] = zero
                field[k, comp, half, PAD + WIN : ROWS, :] = zero


def first_terms(place, src, rec, field, raw, sem):
    start = pl.multiple_of(place[4], 8)
    loads = []
    for n, ref in enumerate((src, rec)):
        cp = pltpu.make_async_copy(ref.at[0, :, pl.ds(start, WIN), :], raw.at[n], sem.at[n])
        cp.start()
        loads.append(cp)
    clear_ends(field)
    for n in range(2):
        loads[n].wait()
        for part in range(2):
            for tile in range(STEPS):
                r = 8 * tile
                lo, hi = raw[n, part, r : r + 8, 0:LANES], raw[n, part, r : r + 8, LANES:NY]
                for half, v in enumerate(by_parity(lo, hi)):
                    field[0, 2 * n + part, half, PAD + r : PAD + r + 8, :] = v
    stencils(field)


def all_levels(place, first, w0, w1, w2, w3, coef, keep, send, field, cls, table):
    q, x_at, y_at, core = place[0], place[1], place[2], place[3]
    for n, ref in enumerate((w0, w1, w2, w3)):
        level = place[8 + n]
        for half in range(HALVES):
            for tile in range(STEPS):
                cls[level, half, 8 * tile : 8 * tile + 8, :] = ref[half, 8 * tile : 8 * tile + 8, :]
    clear_ends(field)
    for n in range(2 * K):
        table[n] = jnp.broadcast_to(coef[n : n + 1, :], (8, LANES))
    mirror = 7 - lax.broadcasted_iota(jnp.int32, (8, LANES), 0)
    base = pl.multiple_of(PAD + CHUNK * q - place[4], 8)

    def finish(level, terms):
        def combine(step, carry):
            places = []
            for part in range(COMBINE):
                r = pl.multiple_of(PAD + 8 * (COMBINE * step + part), 8)
                places += [(half, r) for half in range(HALVES)]

            def look_up(half, r):
                ids = cls[level, half, pl.ds(r - PAD, 8), :]
                return [pick(table[n], ids) for n in range(2 * K)]

            ahead = look_up(*places[0])
            for n, (half, r) in enumerate(places):
                coefs = ahead
                if n + 1 < len(places):
                    ahead = look_up(*places[n + 1])
                p, s = [], []
                for comp in range(4):
                    vals = [terms[k, comp, half, pl.ds(r, 8), :] for k in range(K)]
                    a, b = coefs[0] * vals[0], coefs[K] * vals[0]
                    for k in range(1, K):
                        a = a + coefs[k] * vals[k]
                        b = b + coefs[K + k] * vals[k]
                    p.append(a)
                    s.append(b)
                field[0, 0, half, pl.ds(r, 8), :] = p[0] + s[1]
                field[0, 1, half, pl.ds(r, 8), :] = p[1] - s[0]
                field[0, 2, half, pl.ds(r, 8), :] = p[2] - s[3]
                field[0, 3, half, pl.ds(r, 8), :] = p[3] + s[2]
            return carry

        lax.fori_loop(0, STEPS // COMBINE, combine, 0)
        lb = level >> 1
        e = (level ^ lb) & 1

        def image(step, carry):
            for part in range(IMAGE):
                image_rows(IMAGE * step + part)
            return carry

        def image_rows(m):
            y_o, ix = m & 3, m >> 2
            x_o = 2 * (e ^ (q & 1)) + (ix ^ e)
            dx, dy = (x_o - x_at) & 3, (y_o - y_at) & 3
            for flip, ref in enumerate((keep, send)):
                c_o = core ^ flip
                t = jnp.where(c_o == 0, dx, dy)
                u = jnp.where(c_o == 0, dy, dx)
                at = (t * 4 + u) * 2 + lb
                for row in range(4):
                    x = base + 4 * (2 * m + c_o) + row
                    for half in range(HALVES):
                        s_re, s_im = [pick(field[0, comp, half, pl.ds(x - 3, 8), :], mirror, 0) for comp in (0, 1)]
                        r_re, r_im = [field[0, comp, half, pl.ds(x - 4, 8), :] for comp in (2, 3)]
                        ref[at, half, H * row : H * row + H, :] = s_re * r_re + s_im * r_im

        lax.fori_loop(0, 8 // IMAGE, image, 0)

    finish(0, first)

    def level_body(level, carry):
        stencils(field)
        finish(level, field)
        return carry

    lax.fori_loop(1, Z, level_body, 0)


def last_sum(a, b, out):
    scaling = 64.0 ** -0.5
    for tile in range(4):
        rows = slice(8 * tile, 8 * tile + 8)
        parts = [(a[half, rows, :] + b[half, rows, :]) * scaling for half in range(HALVES)]
        lo, hi = by_column(*parts)
        out[tile, 0, :, 0:LANES] = lo
        out[tile, 0, :, LANES:NY] = hi


SCALARS = pl.BlockSpec(memory_space=pltpu.SMEM)
LOCAL = pl.BlockSpec(memory_space=pltpu.VMEM)
REMOTE = pl.BlockSpec(memory_space=pltpu.HBM)
TERMS = (K, 4, HALVES, ROWS, LANES)
WINDOW = (HALVES, WIN, LANES)


def call(body, outs, ins, scratch=(), flops=0, moved=0):
    return pl.pallas_call(
        body,
        out_shape=[jax.ShapeDtypeStruct(shape, dtype) for shape, dtype in outs],
        in_specs=ins,
        out_specs=[LOCAL] * len(outs),
        scratch_shapes=list(scratch),
        cost_estimate=pl.CostEstimate(flops=flops, bytes_accessed=moved, transcendentals=0),
        compiler_params=pltpu.CompilerParams(vmem_limit_bytes=LIMIT * 2**20),
    )


def in_hbm(array):
    return pltpu.with_memory_space_constraint(array, pltpu.HBM)


def per_device(source, receiver, classes, coef_table, freq_list):
    d = lax.axis_index("depth")
    f = lax.axis_index("freq")
    zh, x_at, y_at, core = f >> 5, (f >> 3) & 3, (f >> 1) & 3, f & 1
    z = 4 * zh + d
    q = chunk_at(z)
    starts = [window_start(chunk_at((z + step) & 7)) for step in (0, 2 - 4 * core, 1, -1)]
    levels = [(d + step) & 3 for step in (0, 2, -1, 1)]
    place = jnp.stack([q, x_at, y_at, core] + starts + levels).astype(jnp.int32)
    own, two, up, down = call(
        cut_windows,
        [(WINDOW, jnp.int32)] * 4,
        [SCALARS, REMOTE],
        [pltpu.VMEM((NX, NY), jnp.int32), pltpu.VMEM((HALVES, NX, LANES), jnp.int32), pltpu.SemaphoreType.DMA((4,))],
    )(place, in_hbm(classes))
    class_windows = [
        own,
        lax.ppermute(two, AXES, along_z(lambda c: 2 if c == 0 else -2)),
        lax.ppermute(up, AXES, along_z(lambda c: 1)),
        lax.ppermute(down, AXES, along_z(lambda c: -1)),
    ]
    mine = lax.dynamic_slice_in_dim(coef_table, freq_list[0], 1, axis=1)[:, 0]
    rows = jnp.transpose(mine, (1, 2, 0)).reshape(2 * K, -1)
    coef = jnp.pad(rows, [(0, 4), (0, LANES - rows.shape[1])])
    (first,) = call(
        first_terms,
        [(TERMS, jnp.float32)],
        [SCALARS, REMOTE, REMOTE],
        [pltpu.VMEM((2, 2, WIN, NY), jnp.float32), pltpu.SemaphoreType.DMA((2,))],
        flops=10**7,
        moved=4 * 2**20,
    )(place, in_hbm(source), in_hbm(receiver))
    half_image = ((32, HALVES, 4 * H, LANES), jnp.float32)
    keep, send = call(
        all_levels,
        [half_image, half_image],
        [SCALARS] + [LOCAL] * 6,
        [
            pltpu.VMEM(TERMS, jnp.float32),
            pltpu.VMEM((Z,) + WINDOW, jnp.int32),
            pltpu.VMEM((2 * K, 8, LANES), jnp.float32),
        ],
        flops=5 * 10**7,
        moved=4 * 2**20,
    )(place, first, *class_windows, coef)

    mine = keep + lax.ppermute(send, AXES, CORE_SWAP)
    for axis in (first_axis, second_axis):
        part = mine.shape[0] // 4
        got = [lax.ppermute(mine[t * part : (t + 1) * part], AXES, axis(t)) for t in (1, 2, 3)]
        mine = mine[:part] + got[0] + got[1] + got[2]
    sent = [lax.dynamic_index_in_dim(mine, p ^ sent_first(q, zh), 0, keepdims=False) for p in (0, 1)]
    got = [lax.ppermute(sent[p], AXES, to_owner(p)) for p in (0, 1)]
    (image,) = call(last_sum, [((4, 1, H, NY), jnp.float32)], [LOCAL, LOCAL])(*got)
    return image


def solution(mesh):
    placed = (
        P("freq", None, None, None),
        P("freq", None, None, None),
        P("depth", None, None),
        P(),
        P("freq"),
    )
    return jax.shard_map(
        per_device,
        mesh=mesh,
        in_specs=placed,
        out_specs=P("freq", "depth", None, None),
        check_vma=False,
    )
```

```python
import functools
import jax
import jax.numpy as jnp
from jax import lax
from jax.experimental import pallas as pl
from jax.experimental.pallas import tpu as pltpu
from jax.sharding import PartitionSpec as P

AXES = ("depth", "freq")
H = 8
K = 6
Z = 4
NX = 256
NY = 256
CHUNK = 64
WIN = 112
HALO = 24
STEPS = WIN // 8
PAD = 8
ROWS = WIN + 2 * PAD
IMAGE = 4
COMPS = 2
LIMIT = 32
LANES = 128
HALVES = NY // LANES


def split(linear):
    d, f = divmod(linear, 64)
    return d, f >> 5, (f >> 3) & 3, (f >> 1) & 3, f & 1


def join(d, zh, x, y, c):
    return d * 64 + ((zh * 4 + x) * 4 + y) * 2 + c


def route(move):
    return [(i, join(*move(*split(i)))) for i in range(256)]


def along_z(step):
    def move(d, zh, x, y, c):
        z = (zh * 4 + d + step(c)) % 8
        return z & 3, z >> 2, x, y, c

    return route(move)


def first_axis(t):
    def move(d, zh, x, y, c):
        return (d, zh, (x + t) % 4, y, c) if c == 0 else (d, zh, x, (y + t) % 4, c)

    return route(move)


def second_axis(t):
    def move(d, zh, x, y, c):
        return (d, zh, x, (y + t) % 4, c) if c == 0 else (d, zh, (x + t) % 4, y, c)

    return route(move)


def chunk_at(z):
    return ((z & 3) + 2 * (z >> 2) + 3) & 3


def sent_first(q, zh):
    return 1 ^ zh ^ (q & 1) ^ (q >> 1)


def to_owner(p):
    def move(d, zh, x, y, c):
        q = chunk_at(4 * zh + d)
        e = (x >> 1) ^ (q & 1)
        level = e ^ (3 * (p ^ sent_first(q, zh)))
        return level, q >> 1, 2 * (q & 1) + ((x & 1) ^ e), y, c

    return route(move)


CORE_SWAP = route(lambda d, zh, x, y, c: (d, zh, x, y, 1 - c))


def window_start(q):
    return jnp.clip(CHUNK * q - HALO, 0, NX - WIN)


def lanes_of(shape=(8, LANES)):
    return lax.broadcasted_iota(jnp.int32, shape, 1)


def pick(v, ids, axis=1):
    return jnp.take_along_axis(v, ids, axis=axis, mode="promise_in_bounds")


def by_parity(lo, hi):
    lane = lanes_of()
    even = (2 * lane) & (LANES - 1)
    low = lane < LANES // 2
    return tuple(jnp.where(low, pick(lo, even + p), pick(hi, even + p)) for p in (0, 1))


def by_column(even, odd):
    lane = lanes_of()
    is_odd = (lane & 1) == 1
    return tuple(
        jnp.where(is_odd, pick(odd, (lane >> 1) + base), pick(even, (lane >> 1) + base)) for base in (0, LANES // 2)
    )


def cut_windows(place, classes, src, rec, own, two, up, down, fields, raw, parted, sem, field_sem):
    here = pl.multiple_of(place[4], 8)
    quarter = NX // 4
    loads = []
    for n in range(4):
        rows = pl.ds(quarter * n, quarter)
        cp = pltpu.make_async_copy(classes.at[0, rows, :], raw.at[rows, :], sem.at[n])
        cp.start()
        loads.append(cp)
    field_loads = []
    for n, ref in enumerate((src, rec)):
        cp = pltpu.make_async_copy(ref.at[0, :, pl.ds(here, WIN), :], fields.at[n], field_sem.at[n])
        cp.start()
        field_loads.append(cp)
    for n in range(4):
        loads[n].wait()
        for r in range(quarter * n, quarter * (n + 1), 8):
            for half, v in enumerate(by_parity(raw[r : r + 8, 0:LANES], raw[r : r + 8, LANES:NY])):
                parted[half, r : r + 8, :] = v
    for n, ref in enumerate((own, two, up, down)):
        start = pl.multiple_of(place[4 + n], 8)
        for half in range(HALVES):
            for tile in range(STEPS):
                ref[half, 8 * tile : 8 * tile + 8, :] = parted[half, pl.ds(start + 8 * tile, 8), :]
    for cp in field_loads:
        cp.wait()


def stencil(field, comp, tiles, top):
    lane = lanes_of()
    first_lane, last_lane = lane == 0, lane == LANES - 1
    for k in range(1, K):
        for tile in range(tiles):
            at = pl.multiple_of(PAD + top, 8) + 8 * tile if not isinstance(top, int) else PAD + top + 8 * tile
            g, rest = [], []
            for half in range(HALVES):
                v = field[k - 1, comp, half, pl.ds(at, 8), :]
                h = 0.5 * (field[k - 1, comp, half, pl.ds(at - 1, 8), :] + field[k - 1, comp, half, pl.ds(at + 1, 8), :])
                g.append(h + v)
                rest.append(h - v)
            before = jnp.where(first_lane, 0.0, pltpu.roll(g[1], 1, 1))
            after = jnp.where(last_lane, 0.0, pltpu.roll(g[0], LANES - 1, 1))
            sides = (before + g[1], g[0] + after)
            for half in range(HALVES):
                w = 0.5 * sides[half] + rest[half]
                if k == 1:
                    w = 0.5 * w
                else:
                    w = w - field[k - 2, comp, half, pl.ds(at, 8), :]
                field[k, comp, half, pl.ds(at, 8), :] = w


def stencils(field, tiles=STEPS, top=0):
    def some(step, carry):
        for part in range(COMPS):
            stencil(field, COMPS * step + part, tiles, top)
        return carry

    lax.fori_loop(0, 4 // COMPS, some, 0)


def clear_ends(field):
    zero = jnp.zeros((8, LANES), jnp.float32)
    for k in range(K - 1):
        for comp in range(4):
            for half in range(HALVES):
                field[k, comp, half, 0:PAD, :] = zero
                field[k, comp, half, PAD + WIN : ROWS, :] = zero


def first_terms(fields, field):
    clear_ends(field)
    for n in range(2):
        for part in range(2):
            for tile in range(STEPS):
                r = 8 * tile
                lo, hi = fields[n, part, r : r + 8, 0:LANES], fields[n, part, r : r + 8, LANES:NY]
                for half, v in enumerate(by_parity(lo, hi)):
                    field[0, 2 * n + part, half, PAD + r : PAD + r + 8, :] = v
    stencils(field)


def all_levels(place, first, w0, w1, w2, w3, coef, keep, send, field, cls, table):
    q, x_at, y_at, core = place[0], place[1], place[2], place[3]
    for n, ref in enumerate((w0, w1, w2, w3)):
        level = place[8 + n]
        for half in range(HALVES):
            for tile in range(STEPS):
                cls[level, half, 8 * tile : 8 * tile + 8, :] = ref[half, 8 * tile : 8 * tile + 8, :]
    clear_ends(field)
    for n in range(2 * K):
        table[n] = jnp.broadcast_to(coef[n : n + 1, :], (8, LANES))
    mirror = 7 - lax.broadcasted_iota(jnp.int32, (8, LANES), 0)
    base = pl.multiple_of(PAD + CHUNK * q - place[4], 8)

    def finish(level, terms, tiles, top):
        def combine(step, carry):
            places = []
            for part in range(tiles // 2):
                r = pl.multiple_of(PAD + top + 8 * (tiles // 2 * step + part), 8)
                places += [(half, r) for half in range(HALVES)]

            def look_up(half, r):
                ids = cls[level, half, pl.ds(r - PAD, 8), :]
                return [pick(table[n], ids) for n in range(2 * K)]

            ahead = look_up(*places[0])
            for n, (half, r) in enumerate(places):
                coefs = ahead
                if n + 1 < len(places):
                    ahead = look_up(*places[n + 1])
                p, s = [], []
                for comp in range(4):
                    vals = [terms[k, comp, half, pl.ds(r, 8), :] for k in range(K)]
                    a, b = coefs[0] * vals[0], coefs[K] * vals[0]
                    for k in range(1, K):
                        a = a + coefs[k] * vals[k]
                        b = b + coefs[K + k] * vals[k]
                    p.append(a)
                    s.append(b)
                field[0, 0, half, pl.ds(r, 8), :] = p[0] + s[1]
                field[0, 1, half, pl.ds(r, 8), :] = p[1] - s[0]
                field[0, 2, half, pl.ds(r, 8), :] = p[2] - s[3]
                field[0, 3, half, pl.ds(r, 8), :] = p[3] + s[2]
            return carry

        lax.fori_loop(0, 2, combine, 0)
        lb = level >> 1
        e = (level ^ lb) & 1

        def image(step, carry):
            for part in range(IMAGE):
                image_rows(IMAGE * step + part)
            return carry

        def image_rows(m):
            y_o, ix = m & 3, m >> 2
            x_o = 2 * (e ^ (q & 1)) + (ix ^ e)
            dx, dy = (x_o - x_at) & 3, (y_o - y_at) & 3
            for flip, ref in enumerate((keep, send)):
                c_o = core ^ flip
                t = jnp.where(c_o == 0, dx, dy)
                u = jnp.where(c_o == 0, dy, dx)
                at = (t * 4 + u) * 2 + lb
                for row in range(4):
                    x = base + 4 * (2 * m + c_o) + row
                    for half in range(HALVES):
                        s_re, s_im = [pick(field[0, comp, half, pl.ds(x - 3, 8), :], mirror, 0) for comp in (0, 1)]
                        r_re, r_im = [field[0, comp, half, pl.ds(x - 4, 8), :] for comp in (2, 3)]
                        ref[at, half, H * row : H * row + H, :] = s_re * r_re + s_im * r_im

        lax.fori_loop(0, 8 // IMAGE, image, 0)

    def reach(rows):
        tiles = (CHUNK + 2 * rows) // 8
        return tiles, jnp.clip(CHUNK * q - place[4] - rows, 0, WIN - 8 * tiles)

    finish(0, first, STEPS, 0)
    stencils(field)
    finish(1, field, *reach(16))
    stencils(field, *reach(16))
    finish(2, field, *reach(16))
    stencils(field, *reach(8))
    finish(3, field, *reach(8))


def last_sum(a, b, out):
    scaling = 64.0 ** -0.5
    for tile in range(4):
        rows = slice(8 * tile, 8 * tile + 8)
        parts = [(a[half, rows, :] + b[half, rows, :]) * scaling for half in range(HALVES)]
        lo, hi = by_column(*parts)
        out[tile, 0, :, 0:LANES] = lo
        out[tile, 0, :, LANES:NY] = hi


SCALARS = pl.BlockSpec(memory_space=pltpu.SMEM)
LOCAL = pl.BlockSpec(memory_space=pltpu.VMEM)
REMOTE = pl.BlockSpec(memory_space=pltpu.HBM)
TERMS = (K, 4, HALVES, ROWS, LANES)
WINDOW = (HALVES, WIN, LANES)


def call(body, outs, ins, scratch=(), flops=0, moved=0):
    return pl.pallas_call(
        body,
        out_shape=[jax.ShapeDtypeStruct(shape, dtype) for shape, dtype in outs],
        in_specs=ins,
        out_specs=[LOCAL] * len(outs),
        scratch_shapes=list(scratch),
        cost_estimate=pl.CostEstimate(flops=flops, bytes_accessed=moved, transcendentals=0),
        compiler_params=pltpu.CompilerParams(vmem_limit_bytes=LIMIT * 2**20),
    )


def in_hbm(array):
    return pltpu.with_memory_space_constraint(array, pltpu.HBM)


def per_device(source, receiver, classes, coef_table, freq_list):
    d = lax.axis_index("depth")
    f = lax.axis_index("freq")
    zh, x_at, y_at, core = f >> 5, (f >> 3) & 3, (f >> 1) & 3, f & 1
    z = 4 * zh + d
    q = chunk_at(z)
    starts = [window_start(chunk_at((z + step) & 7)) for step in (0, 2 - 4 * core, 1, -1)]
    levels = [(d + step) & 3 for step in (0, 2, -1, 1)]
    place = jnp.stack([q, x_at, y_at, core] + starts + levels).astype(jnp.int32)
    own, two, up, down, fields = call(
        cut_windows,
        [(WINDOW, jnp.int32)] * 4 + [((2, 2, WIN, NY), jnp.float32)],
        [SCALARS] + [REMOTE] * 3,
        [
            pltpu.VMEM((NX, NY), jnp.int32),
            pltpu.VMEM((HALVES, NX, LANES), jnp.int32),
            pltpu.SemaphoreType.DMA((4,)),
            pltpu.SemaphoreType.DMA((2,)),
        ],
    )(place, in_hbm(classes), in_hbm(source), in_hbm(receiver))
    class_windows = [
        own,
        lax.ppermute(two, AXES, along_z(lambda c: 2 if c == 0 else -2)),
        lax.ppermute(up, AXES, along_z(lambda c: 1)),
        lax.ppermute(down, AXES, along_z(lambda c: -1)),
    ]
    mine = lax.dynamic_slice_in_dim(coef_table, freq_list[0], 1, axis=1)[:, 0]
    rows = jnp.transpose(mine, (1, 2, 0)).reshape(2 * K, -1)
    coef = jnp.pad(rows, [(0, 4), (0, LANES - rows.shape[1])])
    (first,) = call(
        first_terms,
        [(TERMS, jnp.float32)],
        [LOCAL],
        flops=10**7,
        moved=4 * 2**20,
    )(fields)
    half_image = ((32, HALVES, 4 * H, LANES), jnp.float32)
    keep, send = call(
        all_levels,
        [half_image, half_image],
        [SCALARS] + [LOCAL] * 6,
        [
            pltpu.VMEM(TERMS, jnp.float32),
            pltpu.VMEM((Z,) + WINDOW, jnp.int32),
            pltpu.VMEM((2 * K, 8, LANES), jnp.float32),
        ],
        flops=5 * 10**7,
        moved=4 * 2**20,
    )(place, first, *class_windows, coef)

    mine = keep + lax.ppermute(send, AXES, CORE_SWAP)
    for axis in (first_axis, second_axis):
        part = mine.shape[0] // 4
        got = [lax.ppermute(mine[t * part : (t + 1) * part], AXES, axis(t)) for t in (1, 2, 3)]
        mine = mine[:part] + got[0] + got[1] + got[2]
    sent = [lax.dynamic_index_in_dim(mine, p ^ sent_first(q, zh), 0, keepdims=False) for p in (0, 1)]
    got = [lax.ppermute(sent[p], AXES, to_owner(p)) for p in (0, 1)]
    (image,) = call(last_sum, [((4, 1, H, NY), jnp.float32)], [LOCAL, LOCAL])(*got)
    return image


def solution(mesh):
    placed = (
        P("freq", None, None, None),
        P("freq", None, None, None),
        P("depth", None, None),
        P(),
        P("freq"),
    )
    return jax.shard_map(
        per_device,
        mesh=mesh,
        in_specs=placed,
        out_specs=P("freq", "depth", None, None),
        check_vma=False,
    )
```

```python
import functools
import jax
import jax.numpy as jnp
from jax import lax
from jax.experimental import pallas as pl
from jax.experimental.pallas import tpu as pltpu
from jax.sharding import PartitionSpec as P

AXES = ("depth", "freq")
H = 8
K = 6
Z = 4
NX = 256
NY = 256
CHUNK = 64
WIN = 112
HALO = 24
STEPS = WIN // 8
PAD = 8
ROWS = WIN + 2 * PAD
IMAGE = 8
LIMIT = 32
LANES = 128
HALVES = NY // LANES


def split(linear):
    d, f = divmod(linear, 64)
    return d, f >> 5, (f >> 3) & 3, (f >> 1) & 3, f & 1


def join(d, zh, x, y, c):
    return d * 64 + ((zh * 4 + x) * 4 + y) * 2 + c


def route(move):
    return [(i, join(*move(*split(i)))) for i in range(256)]


def along_z(step):
    def move(d, zh, x, y, c):
        z = (zh * 4 + d + step(c)) % 8
        return z & 3, z >> 2, x, y, c

    return route(move)


def first_axis(t):
    def move(d, zh, x, y, c):
        return (d, zh, (x + t) % 4, y, c) if c == 0 else (d, zh, x, (y + t) % 4, c)

    return route(move)


def second_axis(t):
    def move(d, zh, x, y, c):
        return (d, zh, x, (y + t) % 4, c) if c == 0 else (d, zh, (x + t) % 4, y, c)

    return route(move)


def chunk_at(z):
    return ((z & 3) + 2 * (z >> 2) + 3) & 3


def sent_first(q, zh):
    return 1 ^ zh ^ (q & 1) ^ (q >> 1)


def to_owner(p):
    def move(d, zh, x, y, c):
        q = chunk_at(4 * zh + d)
        e = (x >> 1) ^ (q & 1)
        level = e ^ (3 * (p ^ sent_first(q, zh)))
        return level, q >> 1, 2 * (q & 1) + ((x & 1) ^ e), y, c

    return route(move)


CORE_SWAP = route(lambda d, zh, x, y, c: (d, zh, x, y, 1 - c))


def window_start(q):
    return jnp.clip(CHUNK * q - HALO, 0, NX - WIN)


def lanes_of(shape=(8, LANES)):
    return lax.broadcasted_iota(jnp.int32, shape, 1)


def pick(v, ids, axis=1):
    return jnp.take_along_axis(v, ids, axis=axis, mode="promise_in_bounds")


def by_parity(lo, hi):
    lane = lanes_of()
    even = (2 * lane) & (LANES - 1)
    low = lane < LANES // 2
    return tuple(jnp.where(low, pick(lo, even + p), pick(hi, even + p)) for p in (0, 1))


def by_column(even, odd):
    lane = lanes_of()
    is_odd = (lane & 1) == 1
    return tuple(
        jnp.where(is_odd, pick(odd, (lane >> 1) + base), pick(even, (lane >> 1) + base)) for base in (0, LANES // 2)
    )


def cut_windows(place, classes, src, rec, own, two, up, down, fields, raw, parted, sem, field_sem):
    here = pl.multiple_of(place[4], 8)
    quarter = NX // 4
    loads = []
    for n in range(4):
        rows = pl.ds(quarter * n, quarter)
        cp = pltpu.make_async_copy(classes.at[0, rows, :], raw.at[rows, :], sem.at[n])
        cp.start()
        loads.append(cp)
    field_loads = []
    for n, ref in enumerate((src, rec)):
        cp = pltpu.make_async_copy(ref.at[0, :, pl.ds(here, WIN), :], fields.at[n], field_sem.at[n])
        cp.start()
        field_loads.append(cp)
    for n in range(4):
        loads[n].wait()
        for r in range(quarter * n, quarter * (n + 1), 8):
            for half, v in enumerate(by_parity(raw[r : r + 8, 0:LANES], raw[r : r + 8, LANES:NY])):
                parted[half, r : r + 8, :] = v
    for n, ref in enumerate((own, two, up, down)):
        start = pl.multiple_of(place[4 + n], 8)
        for half in range(HALVES):
            for tile in range(STEPS):
                ref[half, 8 * tile : 8 * tile + 8, :] = parted[half, pl.ds(start + 8 * tile, 8), :]
    for cp in field_loads:
        cp.wait()


def stencil(field, comp, tiles, top):
    lane = lanes_of()
    first_lane, last_lane = lane == 0, lane == LANES - 1
    for k in range(1, K):
        for tile in range(tiles):
            at = pl.multiple_of(PAD + top, 8) + 8 * tile if not isinstance(top, int) else PAD + top + 8 * tile
            g, rest = [], []
            for half in range(HALVES):
                v = field[k - 1, comp, half, pl.ds(at, 8), :]
                h = 0.5 * (field[k - 1, comp, half, pl.ds(at - 1, 8), :] + field[k - 1, comp, half, pl.ds(at + 1, 8), :])
                g.append(h + v)
                rest.append(h - v)
            before = jnp.where(first_lane, 0.0, pltpu.roll(g[1], 1, 1))
            after = jnp.where(last_lane, 0.0, pltpu.roll(g[0], LANES - 1, 1))
            sides = (before + g[1], g[0] + after)
            for half in range(HALVES):
                w = 0.5 * sides[half] + rest[half]
                if k == 1:
                    w = 0.5 * w
                else:
                    w = w - field[k - 2, comp, half, pl.ds(at, 8), :]
                field[k, comp, half, pl.ds(at, 8), :] = w


def stencils(field, tiles=STEPS, top=0, together=4):
    def some(step, carry):
        for part in range(together):
            stencil(field, together * step + part, tiles, top)
        return carry

    lax.fori_loop(0, 4 // together, some, 0)


def clear_ends(field):
    zero = jnp.zeros((8, LANES), jnp.float32)
    for k in range(K - 1):
        for comp in range(4):
            for half in range(HALVES):
                field[k, comp, half, 0:PAD, :] = zero
                field[k, comp, half, PAD + WIN : ROWS, :] = zero


def first_terms(fields, field):
    clear_ends(field)
    for n in range(2):
        for part in range(2):
            for tile in range(STEPS):
                r = 8 * tile
                lo, hi = fields[n, part, r : r + 8, 0:LANES], fields[n, part, r : r + 8, LANES:NY]
                for half, v in enumerate(by_parity(lo, hi)):
                    field[0, 2 * n + part, half, PAD + r : PAD + r + 8, :] = v
    stencils(field, together=2)


def all_levels(place, first, w0, w1, w2, w3, coef, keep, send, field, cls, table):
    q, x_at, y_at, core = place[0], place[1], place[2], place[3]
    for n, ref in enumerate((w0, w1, w2, w3)):
        level = place[8 + n]
        for half in range(HALVES):
            for tile in range(STEPS):
                cls[level, half, 8 * tile : 8 * tile + 8, :] = ref[half, 8 * tile : 8 * tile + 8, :]
    clear_ends(field)
    for n in range(2 * K):
        table[n] = jnp.broadcast_to(coef[n : n + 1, :], (8, LANES))
    mirror = 7 - lax.broadcasted_iota(jnp.int32, (8, LANES), 0)
    base = pl.multiple_of(PAD + CHUNK * q - place[4], 8)

    def finish(level, terms, tiles, top):
        def combine(step, carry):
            places = []
            for part in range(tiles):
                r = pl.multiple_of(PAD + top + 8 * (tiles * step + part), 8)
                places += [(half, r) for half in range(HALVES)]

            def look_up(half, r):
                ids = cls[level, half, pl.ds(r - PAD, 8), :]
                return [pick(table[n], ids) for n in range(2 * K)]

            ahead = look_up(*places[0])
            for n, (half, r) in enumerate(places):
                coefs = ahead
                if n + 1 < len(places):
                    ahead = look_up(*places[n + 1])
                p, s = [], []
                for comp in range(4):
                    vals = [terms[k, comp, half, pl.ds(r, 8), :] for k in range(K)]
                    a, b = coefs[0] * vals[0], coefs[K] * vals[0]
                    for k in range(1, K):
                        a = a + coefs[k] * vals[k]
                        b = b + coefs[K + k] * vals[k]
                    p.append(a)
                    s.append(b)
                field[0, 0, half, pl.ds(r, 8), :] = p[0] + s[1]
                field[0, 1, half, pl.ds(r, 8), :] = p[1] - s[0]
                field[0, 2, half, pl.ds(r, 8), :] = p[2] - s[3]
                field[0, 3, half, pl.ds(r, 8), :] = p[3] + s[2]
            return carry

        combine(0, 0)
        lb = level >> 1
        e = (level ^ lb) & 1

        def image(step, carry):
            for part in range(IMAGE):
                image_rows(IMAGE * step + part)
            return carry

        def image_rows(m):
            y_o, ix = m & 3, m >> 2
            x_o = 2 * (e ^ (q & 1)) + (ix ^ e)
            dx, dy = (x_o - x_at) & 3, (y_o - y_at) & 3
            for flip, ref in enumerate((keep, send)):
                c_o = core ^ flip
                t = jnp.where(c_o == 0, dx, dy)
                u = jnp.where(c_o == 0, dy, dx)
                at = (t * 4 + u) * 2 + lb
                for row in range(4):
                    x = base + 4 * (2 * m + c_o) + row
                    for half in range(HALVES):
                        s_re, s_im = [pick(field[0, comp, half, pl.ds(x - 3, 8), :], mirror, 0) for comp in (0, 1)]
                        r_re, r_im = [field[0, comp, half, pl.ds(x - 4, 8), :] for comp in (2, 3)]
                        ref[at, half, H * row : H * row + H, :] = s_re * r_re + s_im * r_im

        lax.fori_loop(0, 8 // IMAGE, image, 0)

    def reach(rows):
        tiles = (CHUNK + 2 * rows) // 8
        return tiles, jnp.clip(CHUNK * q - place[4] - rows, 0, WIN - 8 * tiles)

    finish(0, first, STEPS, 0)
    stencils(field)
    finish(1, field, *reach(16))
    stencils(field, *reach(16))
    finish(2, field, *reach(16))
    stencils(field, *reach(8))
    finish(3, field, *reach(8))


def last_sum(a, b, out):
    scaling = 64.0 ** -0.5
    for tile in range(4):
        rows = slice(8 * tile, 8 * tile + 8)
        parts = [(a[half, rows, :] + b[half, rows, :]) * scaling for half in range(HALVES)]
        lo, hi = by_column(*parts)
        out[tile, 0, :, 0:LANES] = lo
        out[tile, 0, :, LANES:NY] = hi


SCALARS = pl.BlockSpec(memory_space=pltpu.SMEM)
LOCAL = pl.BlockSpec(memory_space=pltpu.VMEM)
REMOTE = pl.BlockSpec(memory_space=pltpu.HBM)
TERMS = (K, 4, HALVES, ROWS, LANES)
WINDOW = (HALVES, WIN, LANES)


def call(body, outs, ins, scratch=(), flops=0, moved=0):
    return pl.pallas_call(
        body,
        out_shape=[jax.ShapeDtypeStruct(shape, dtype) for shape, dtype in outs],
        in_specs=ins,
        out_specs=[LOCAL] * len(outs),
        scratch_shapes=list(scratch),
        cost_estimate=pl.CostEstimate(flops=flops, bytes_accessed=moved, transcendentals=0),
        compiler_params=pltpu.CompilerParams(vmem_limit_bytes=LIMIT * 2**20),
    )


def in_hbm(array):
    return pltpu.with_memory_space_constraint(array, pltpu.HBM)


def per_device(source, receiver, classes, coef_table, freq_list):
    d = lax.axis_index("depth")
    f = lax.axis_index("freq")
    zh, x_at, y_at, core = f >> 5, (f >> 3) & 3, (f >> 1) & 3, f & 1
    z = 4 * zh + d
    q = chunk_at(z)
    starts = [window_start(chunk_at((z + step) & 7)) for step in (0, 2 - 4 * core, 1, -1)]
    levels = [(d + step) & 3 for step in (0, 2, -1, 1)]
    place = jnp.stack([q, x_at, y_at, core] + starts + levels).astype(jnp.int32)
    own, two, up, down, fields = call(
        cut_windows,
        [(WINDOW, jnp.int32)] * 4 + [((2, 2, WIN, NY), jnp.float32)],
        [SCALARS] + [REMOTE] * 3,
        [
            pltpu.VMEM((NX, NY), jnp.int32),
            pltpu.VMEM((HALVES, NX, LANES), jnp.int32),
            pltpu.SemaphoreType.DMA((4,)),
            pltpu.SemaphoreType.DMA((2,)),
        ],
    )(place, in_hbm(classes), in_hbm(source), in_hbm(receiver))
    class_windows = [
        own,
        lax.ppermute(two, AXES, along_z(lambda c: 2 if c == 0 else -2)),
        lax.ppermute(up, AXES, along_z(lambda c: 1)),
        lax.ppermute(down, AXES, along_z(lambda c: -1)),
    ]
    mine = lax.dynamic_slice_in_dim(coef_table, freq_list[0], 1, axis=1)[:, 0]
    rows = jnp.transpose(mine, (1, 2, 0)).reshape(2 * K, -1)
    coef = jnp.pad(rows, [(0, 4), (0, LANES - rows.shape[1])])
    (first,) = call(
        first_terms,
        [(TERMS, jnp.float32)],
        [LOCAL],
        flops=10**7,
        moved=4 * 2**20,
    )(fields)
    half_image = ((32, HALVES, 4 * H, LANES), jnp.float32)
    keep, send = call(
        all_levels,
        [half_image, half_image],
        [SCALARS] + [LOCAL] * 6,
        [
            pltpu.VMEM(TERMS, jnp.float32),
            pltpu.VMEM((Z,) + WINDOW, jnp.int32),
            pltpu.VMEM((2 * K, 8, LANES), jnp.float32),
        ],
        flops=5 * 10**7,
        moved=4 * 2**20,
    )(place, first, *class_windows, coef)

    mine = keep + lax.ppermute(send, AXES, CORE_SWAP)
    for axis in (first_axis, second_axis):
        part = mine.shape[0] // 4
        got = [lax.ppermute(mine[t * part : (t + 1) * part], AXES, axis(t)) for t in (1, 2, 3)]
        mine = mine[:part] + got[0] + got[1] + got[2]
    sent = [lax.dynamic_index_in_dim(mine, p ^ sent_first(q, zh), 0, keepdims=False) for p in (0, 1)]
    got = [lax.ppermute(sent[p], AXES, to_owner(p)) for p in (0, 1)]
    (image,) = call(last_sum, [((4, 1, H, NY), jnp.float32)], [LOCAL, LOCAL])(*got)
    return image


def solution(mesh):
    placed = (
        P("freq", None, None, None),
        P("freq", None, None, None),
        P("depth", None, None),
        P(),
        P("freq"),
    )
    return jax.shard_map(
        per_device,
        mesh=mesh,
        in_specs=placed,
        out_specs=P("freq", "depth", None, None),
        check_vma=False,
    )
```
